32 devices in a mesh: section: 2 (over core), space: 16 (over z, y, x).
Axes of the slice: x: 2, y: 2, z: 4, core: 2. Of those that a mesh axis runs over, the one named last changes fastest.
Arguments:
- feats: bfloat16 [2, 384, 128, 128], P('section', 'space'), may hold values from -6 to 6
- w_first: bfloat16 [2, 27, 128, 128], P('section'), may hold values from -0.109375 to 0.109375
- w_second: bfloat16 [2, 27, 128, 128], P('section'), may hold values from -0.109375 to 0.109375
- w_skip: bfloat16 [27, 128, 128], replicated, may hold values from -0.109375 to 0.109375
- send_tiles: int32 [2, 128, 2], P('section', 'space'), may hold values from 0 to 23
- send_counts: int32 [2, 128], P('section', 'space'), may hold values from 0 to 2, as said below
- neighbours: int32 [2, 27, 384], P('section', None, 'space'), may hold values from 0 to 40, as said below
Outputs:
- outputs: bfloat16 [2, 384, 128, 128], P('section', 'space')
The draws below stay inside these ranges and needn't reach their ends.
Inputs may be any that keep to these rules, and one draw needn't show every extreme that they name: `send_tiles`: entry [s, p * 8 + d, j] names one of partition p's own tiles. `send_counts`: entry [s, p * 8 + d] is how many slots partition p fills toward its neighbour in direction d; 0 where that neighbour lies outside the grid. `neighbours`: for output tile t of partition q, a value below 24 is q's own tile, 24 + d * 2 + j is slot j of direction d in q's table, 40 is no neighbour; offset 13 names tile t itself.
All inputs are finite; a program needn't handle non-finite values.
Results may differ from the reference program's by a relative error of at most 0.0049.
Values may be sent and summed in bfloat16 or wider, within the bound.
A program may use at most 64 MiB of HBM per device.

```python
import math
import jax
import jax.numpy as jnp
from jax import lax

C = 128
VOX = 128
KOFF = 27
DIRS = 8
CAP = 2
GRID_B = 8
TILES = 24
GRID_A = 2
PARTITIONS = 16
TILES_ALL = 384
OUTBOX = 128
SLOTS = 16
EMPTY = 40


step_rows = (-1, -1, -1, 0, 0, 1, 1, 1)


step_cols = (-1, 0, 1, -1, 1, -1, 0, 1)


def draw_send_counts(key, part):
    partition = jnp.arange(PARTITIONS, dtype=jnp.int32)[:, None]
    grid_row = partition // GRID_B + jnp.array(step_rows, dtype=jnp.int32)[None, :]
    grid_col = partition % GRID_B + jnp.array(step_cols, dtype=jnp.int32)[None, :]
    inside = (grid_row >= 0) & (grid_row < GRID_A) & (grid_col >= 0) & (grid_col < GRID_B)
    counts = jax.random.randint(jax.random.fold_in(key, 11), (2, PARTITIONS, DIRS), 0, CAP + 1, dtype=jnp.int32)
    counts = jnp.where(inside[None], counts, 0)
    counts = counts.at[:, 0, 7].set(CAP)
    return counts.reshape(2, OUTBOX)


def draw_neighbours(key, part):
    full_shape = (2, KOFF, TILES_ALL)
    local_ids = jax.random.randint(jax.random.fold_in(key, 21), full_shape, 0, TILES, dtype=jnp.int32)
    remote_ids = jax.random.randint(jax.random.fold_in(key, 22), full_shape, TILES, EMPTY, dtype=jnp.int32)
    picker = jax.random.randint(jax.random.fold_in(key, 23), full_shape, 0, 20, dtype=jnp.int32)
    chosen = jnp.where(picker < 14, local_ids, jnp.where(picker < 19, remote_ids, EMPTY))
    centre = jnp.arange(TILES_ALL, dtype=jnp.int32) % TILES
    return chosen.at[:, 13, :].set(jnp.broadcast_to(centre, (2, TILES_ALL)))


def plant(values, rng, low, high):
    longest = values.shape.index(max(values.shape))
    spots = []
    for shift in (0, 1):
        where = [jax.random.randint(jax.random.fold_in(rng, axis), (), 0, length) for axis, length in enumerate(values.shape)]
        where[longest] = (where[longest] + shift) % values.shape[longest]
        spots.append(tuple(where))
    return values.at[spots[0]].set(low).at[spots[1]].set(high)


def shard_levels(own_key, shape, pieces, smallest, top_value):
    def one(dim, parts):
        heights = jax.random.uniform(jax.random.fold_in(jax.random.fold_in(own_key, 6), dim), (parts,), jnp.float32, smallest / len(pieces), top_value / len(pieces))
        return jnp.repeat(jnp.exp(heights), shape[dim] // parts).reshape((-1,) + (1,) * (len(shape) - dim - 1))

    loudness = one(*pieces[0])
    for cut in pieces[1:]:
        loudness = loudness * one(*cut)
    return loudness


def gaussian(rng, shape, spread, reach, split=(), held_as=jnp.bfloat16):
    factor_of = shard_levels(rng, shape, split, -0.22, 0.18) if split else 1.0
    drawn = jax.random.normal(rng, shape, jnp.float32) * spread * factor_of
    return jnp.minimum(jnp.maximum(drawn, -reach), reach).astype(held_as)


def setup_inputs(seed: int = 0) -> dict:
    keys = jax.random.split(jax.random.key(seed), 8)
    feats = gaussian(keys[0], (2, TILES_ALL, C, VOX), 1.0, 6.0, ((0, 2), (1, 16)))
    w_first = gaussian(keys[1], (2, KOFF, C, C), (KOFF * C) ** -0.5, 0.109375, ((0, 2),))
    w_second = gaussian(keys[2], (2, KOFF, C, C), (KOFF * C) ** -0.5, 0.109375, ((0, 2),))
    w_skip = gaussian(keys[3], (KOFF, C, C), (KOFF * C) ** -0.5, 0.109375)
    send_tiles = plant(jax.random.randint(keys[4], (2, OUTBOX, CAP), 0, TILES), jax.random.fold_in(keys[4], 1), 0, TILES - 1).astype(jnp.int32)
    send_counts = draw_send_counts(jax.random.fold_in(keys[7], 71), 0)
    neighbours = draw_neighbours(jax.random.fold_in(keys[7], 71), 0)
    return {"feats": feats, "w_first": w_first, "w_second": w_second, "w_skip": w_skip, "send_tiles": send_tiles, "send_counts": send_counts, "neighbours": neighbours}


step_rows = (-1, -1, -1, 0, 0, 1, 1, 1)
step_cols = (-1, 0, 1, -1, 1, -1, 0, 1)


def tile_conv(tile_table, tile_ids, weights):
    block_width = math.gcd(TILES, 8)
    grouped = tile_ids.T.reshape(TILES // block_width, block_width, KOFF)
    float_weights = weights.astype(jnp.float32)

    def one_block(block_ids):
        gathered = tile_table[block_ids].astype(jnp.float32)
        return jnp.einsum("koc,bkcv->bov", float_weights, gathered, precision=lax.Precision.HIGHEST)

    result = lax.map(one_block, grouped)
    return result.reshape(TILES, C, VOX)


def section_conv(tile_field, weights, send_rows, counts, tile_ids):
    rows_grid = send_rows.reshape(PARTITIONS, DIRS, CAP)
    count_grid = counts.reshape(PARTITIONS, DIRS)
    step_a = jnp.array(step_rows, dtype=jnp.int32)
    step_b = jnp.array(step_cols, dtype=jnp.int32)
    zero_tile = jnp.zeros((1,) + tile_field.shape[1:], tile_field.dtype)
    direction_ids = jnp.arange(DIRS, dtype=jnp.int32)

    def one_device(device):
        own_tiles = lax.dynamic_slice_in_dim(tile_field, device * TILES, TILES, 0)
        grid_row = device // GRID_B - step_a
        grid_col = device % GRID_B - step_b
        inside = (grid_row >= 0) & (grid_row < GRID_A) & (grid_col >= 0) & (grid_col < GRID_B)
        source = jnp.where(inside, grid_row * GRID_B + grid_col, 0).astype(jnp.int32)
        chosen = rows_grid[source, direction_ids]
        live_counts = jnp.where(inside, count_grid[source, direction_ids], 0)
        picked = tile_field[source[:, None] * TILES + chosen]
        live_slot = jnp.arange(CAP, dtype=jnp.int32)[None, :] < live_counts[:, None]
        picked = jnp.where(live_slot[:, :, None, None], picked, jnp.zeros_like(picked))
        tile_table = jnp.concatenate([own_tiles, picked.reshape((SLOTS,) + tile_field.shape[1:]), zero_tile], axis=0)
        local_ids = lax.dynamic_slice_in_dim(tile_ids, device * TILES, TILES, 1)
        return tile_conv(tile_table, local_ids, weights)

    result = lax.map(one_device, jnp.arange(PARTITIONS, dtype=jnp.int32))
    return result.reshape(TILES_ALL, C, VOX)


def reference(feats, w_first, w_second, w_skip, send_tiles, send_counts, neighbours):
    encoder_first = jax.nn.relu(section_conv(feats[0], w_first[0], send_tiles[0], send_counts[0], neighbours[0])).astype(jnp.bfloat16)
    decoder_first = jax.nn.relu(section_conv(feats[1], w_first[1], send_tiles[1], send_counts[1], neighbours[1])).astype(jnp.bfloat16)
    decoder_input = jnp.concatenate([decoder_first, encoder_first], axis=1)
    decoder_weights = jnp.concatenate([w_second[1], w_skip], axis=2)
    encoder_out = jax.nn.relu(section_conv(encoder_first, w_second[0], send_tiles[0], send_counts[0], neighbours[0])).astype(jnp.bfloat16)
    decoder_out = jax.nn.relu(section_conv(decoder_input, decoder_weights, send_tiles[1], send_counts[1], neighbours[1])).astype(jnp.bfloat16)
    return jnp.stack([encoder_out, decoder_out])
```

```python
import jax
import jax.numpy as jnp
from jax import lax
from jax.experimental import pallas as pl
from jax.experimental.pallas import tpu as pltpu
from jax.sharding import PartitionSpec as P

GRID_B = 8

step_rows = (-1, -1, -1, 0, 0, 1, 1, 1)
step_cols = (-1, 0, 1, -1, 1, -1, 0, 1)


def shifted(block, axis, distance):
    devices = range(lax.axis_size(axis))
    route = [(i - distance, i) for i in devices if i - distance in devices]
    return lax.ppermute(block, axis, route)


def conv_tiles(ids, pairs, emit, tiles, koff):
    def body(step, _):
        t = step * 2
        terms = [(w, table, k) for k in range(koff) for w, table in pairs]
        acc = None
        for i in range(0, len(terms), 2):
            lhs, rhs = [], []
            for w, table, k in terms[i : i + 2]:
                lhs.append(w[k])
                rhs.append(jnp.concatenate([table[ids[k, t]], table[ids[k, t + 1]]], axis=1))
            part = jnp.dot(
                jnp.concatenate(lhs, axis=1),
                jnp.concatenate(rhs, axis=0),
                preferred_element_type=jnp.float32,
            )
            acc = part if acc is None else acc + part
        emit(t, acc)
        return 0

    lax.fori_loop(0, tiles // 2, body, 0)


def fill(table, own, arrived):
    tiles, slots = own.shape[0], arrived.shape[0]
    table[pl.ds(0, tiles)] = own[...]
    table[pl.ds(tiles, slots)] = arrived[...]
    table[tiles + slots] = jnp.zeros(table.shape[1:], table.dtype)


def store_relu(out):
    def emit(t, acc):
        vox = out.shape[2]
        acc = jnp.maximum(acc, 0.0).astype(out.dtype)
        out[t] = acc[:, :vox]
        out[t + 1] = acc[:, vox:]

    return emit


def first_kernel(ids, own, arrived, w, out, table):
    fill(table, own, arrived)
    conv_tiles(ids, [(w, table)], store_relu(out), own.shape[0], w.shape[0])


def second_kernel(ids, own, arrived, skip, skip_arrived, w, w_skip, out, table, skip_table):
    fill(table, own, arrived)

    @pl.when(lax.axis_index("section") == 0)
    def _():
        conv_tiles(ids, [(w, table)], store_relu(out), own.shape[0], w.shape[0])

    @pl.when(lax.axis_index("section") == 1)
    def _():
        fill(skip_table, skip, skip_arrived)
        conv_tiles(
            ids, [(w, table), (w_skip, skip_table)], store_relu(out), own.shape[0], w.shape[0]
        )


def select_kernel(rows, counts, *refs):
    fields, outs = refs[: len(refs) // 2], refs[len(refs) // 2 :]
    for field, out in zip(fields, outs):
        for d in range(rows.shape[0]):
            for j in range(rows.shape[1]):
                tile = field[rows[d, j]]
                out[d, j] = jnp.where(j < counts[d], tile, jnp.zeros_like(tile))


VMEM = pl.BlockSpec(memory_space=pltpu.VMEM)
SMEM = pl.BlockSpec(memory_space=pltpu.SMEM)


def halos(fields, send_rows, counts):
    dirs, cap = send_rows.shape
    tile = fields[0].shape[1:]
    outgoing = pl.pallas_call(
        select_kernel,
        out_shape=[jax.ShapeDtypeStruct((dirs, cap) + tile, f.dtype) for f in fields],
        in_specs=[SMEM, SMEM] + [VMEM] * len(fields),
        out_specs=[VMEM] * len(fields),
    )(send_rows, counts, *fields)
    joined = jnp.stack(outgoing, axis=2)
    groups = []
    for direction in range(len(step_rows)):
        distance = step_rows[direction] * GRID_B + step_cols[direction]
        groups.append(shifted(joined[direction], "space", distance))
    arrived = jnp.stack(groups).reshape((dirs * cap, len(fields)) + tile)
    return [arrived[:, i] for i in range(len(fields))]


def local(feats, w_first, w_second, w_skip, send_tiles, send_counts, neighbours):
    ids, send_rows, counts = neighbours[0], send_tiles[0], send_counts[0]
    own = feats[0]
    tiles, channels, vox = own.shape
    slots = send_rows.shape[0] * send_rows.shape[1]
    table = pltpu.VMEM((tiles + slots + 1, channels, vox), own.dtype)
    shape = jax.ShapeDtypeStruct((tiles, channels, vox), own.dtype)
    (arrived,) = halos([own], send_rows, counts)
    first = pl.pallas_call(
        first_kernel,
        out_shape=shape,
        in_specs=[SMEM] + [VMEM] * 3,
        out_specs=VMEM,
        scratch_shapes=[table],
    )(ids, own, arrived, w_first[0])
    skip = shifted(first, "section", 1)
    arrived, skip_arrived = halos([first, skip], send_rows, counts)
    second = pl.pallas_call(
        second_kernel,
        out_shape=shape,
        in_specs=[SMEM] + [VMEM] * 6,
        out_specs=VMEM,
        scratch_shapes=[table, table],
    )(ids, first, arrived, skip, skip_arrived, w_second[0], w_skip)
    return second[None]


def solution(mesh):
    placed = (
        P("section", "space", None, None),
        P("section", None, None, None),
        P("section", None, None, None),
        P(),
        P("section", "space", None),
        P("section", "space"),
        P("section", None, "space"),
    )
    return jax.shard_map(
        local,
        mesh=mesh,
        in_specs=placed,
        out_specs=P("section", "space", None, None),
        check_vma=False,
    )
```

```python
import jax
import jax.numpy as jnp
from jax import lax
from jax.experimental import pallas as pl
from jax.experimental.pallas import tpu as pltpu
from jax.sharding import PartitionSpec as P

GRID_B = 8

step_rows = (-1, -1, -1, 0, 0, 1, 1, 1)
step_cols = (-1, 0, 1, -1, 1, -1, 0, 1)


def conv_tiles(ids, pairs, emit, tiles, koff):
    def body(step, _):
        t = step * 2
        terms = [(w, table, k) for k in range(koff) for w, table in pairs]
        acc = None
        for i in range(0, len(terms), 2):
            lhs, rhs = [], []
            for w, table, k in terms[i : i + 2]:
                lhs.append(w[k])
                rhs.append(jnp.concatenate([table[ids[k, t]], table[ids[k, t + 1]]], axis=1))
            part = jnp.dot(
                jnp.concatenate(lhs, axis=1),
                jnp.concatenate(rhs, axis=0),
                preferred_element_type=jnp.float32,
            )
            acc = part if acc is None else acc + part
        emit(t, acc)
        return 0

    lax.fori_loop(0, tiles // 2, body, 0)


MESH = pl.DeviceIdType.MESH


def network(
    ids, rows, counts, feats, w1_hbm, w2_hbm, w3_hbm, out,
    table1, table2, table3, w1, w2, w3, acc,
    outbox1, outbox2, outbox3, inbox1, inbox2, inbox3,
    local_sems, send1, recv1, send2, recv2, send3, recv3, send_skip, recv_skip,
):
    tiles, _, vox = feats.shape
    dirs, cap = rows.shape
    koff = w1.shape[0]
    section = lax.axis_index("section")
    me = lax.axis_index("space")
    grid_a = lax.axis_size("space") // GRID_B
    row, col = me // GRID_B, me % GRID_B

    def inside(d, sign):
        r, c = row + sign * step_rows[d], col + sign * step_cols[d]
        return (r >= 0) & (r < grid_a) & (c >= 0) & (c < GRID_B)

    def target(d):
        return {"section": section, "space": me + step_rows[d] * GRID_B + step_cols[d]}

    sibling = {"section": 1 - section, "space": me}

    loads = [
        pltpu.make_async_copy(src, dst, local_sems.at[i])
        for i, (src, dst) in enumerate(
            [(feats, table1.at[pl.ds(0, tiles)]), (w1_hbm, w1), (w2_hbm, w2), (w3_hbm, w3)]
        )
    ]
    for load in loads:
        load.start()

    barrier = pltpu.get_barrier_semaphore()
    for d in range(dirs):

        @pl.when(inside(d, 1))
        def _():
            pl.semaphore_signal(barrier, inc=1, device_id=target(d), device_id_type=MESH)

    pl.semaphore_signal(barrier, inc=1, device_id=sibling, device_id_type=MESH)
    peers = jnp.int32(1)
    for d in range(dirs):
        peers += jnp.where(inside(d, -1), 1, 0).astype(jnp.int32)
    pl.semaphore_wait(barrier, peers)

    def halo_copy(d, outbox, inbox, send, recv):
        return pltpu.make_async_remote_copy(
            src_ref=outbox.at[d],
            dst_ref=inbox.at[d],
            send_sem=send.at[d],
            recv_sem=recv.at[d],
            device_id=target(d),
            device_id_type=MESH,
        )

    def halo_send(table, outbox, inbox, send, recv):
        for d in range(dirs):
            for j in range(cap):
                tile = table[rows[d, j]]
                outbox[d, j] = jnp.where(j < counts[d], tile, jnp.zeros_like(tile))

            @pl.when(inside(d, 1))
            def _():
                halo_copy(d, outbox, inbox, send, recv).start()

    def halo_receive(table, outbox, inbox, send, recv):
        for d in range(dirs):
            place = pl.ds(tiles + d * cap, cap)

            @pl.when(inside(d, -1))
            def _():
                halo_copy(d, outbox, inbox, send, recv).wait_recv()
                table[place] = inbox[d]

            @pl.when(jnp.logical_not(inside(d, -1)))
            def _():
                table[place] = jnp.zeros((cap,) + table.shape[1:], table.dtype)

        table[tiles + dirs * cap] = jnp.zeros(table.shape[1:], table.dtype)

    def halo_sent(outbox, inbox, send, recv):
        for d in range(dirs):

            @pl.when(inside(d, 1))
            def _():
                halo_copy(d, outbox, inbox, send, recv).wait_send()

    def skip_copy(t):
        return pltpu.make_async_remote_copy(
            src_ref=table2.at[pl.ds(t, 2)],
            dst_ref=table3.at[pl.ds(t, 2)],
            send_sem=send_skip.at[t // 2],
            recv_sem=recv_skip.at[t // 2],
            device_id=sibling,
            device_id_type=MESH,
        )

    halo1 = (outbox1, inbox1, send1, recv1)
    halo2 = (outbox2, inbox2, send2, recv2)
    halo3 = (outbox3, inbox3, send3, recv3)

    loads[0].wait()
    halo_send(table1, *halo1)
    halo_receive(table1, *halo1)
    loads[1].wait()

    def emit_first(t, part):
        part = jnp.maximum(part, 0.0).astype(table2.dtype)
        table2[t] = part[:, :vox]
        table2[t + 1] = part[:, vox:]

        @pl.when(section == 0)
        def _():
            skip_copy(t).start()

    conv_tiles(ids, [(w1, table1)], emit_first, tiles, koff)
    halo_send(table2, *halo2)

    @pl.when(section == 1)
    def _():
        lax.fori_loop(0, tiles // 2, lambda i, _: (skip_copy(2 * i).wait_recv(), 0)[1], 0)
        halo_send(table3, *halo3)

    halo_receive(table2, *halo2)
    loads[2].wait()
    loads[3].wait()

    def emit_out(t, part):
        acc[t // 2] = part
        part = jnp.maximum(part, 0.0).astype(out.dtype)
        out[t] = part[:, :vox]
        out[t + 1] = part[:, vox:]

    conv_tiles(ids, [(w2, table2)], emit_out, tiles, koff)

    @pl.when(section == 0)
    def _():
        lax.fori_loop(0, tiles // 2, lambda i, _: (skip_copy(2 * i).wait_send(), 0)[1], 0)

    @pl.when(section == 1)
    def _():
        halo_receive(table3, *halo3)

        def emit_sum(t, part):
            part = jnp.maximum(part + acc[t // 2], 0.0).astype(out.dtype)
            out[t] = part[:, :vox]
            out[t + 1] = part[:, vox:]

        conv_tiles(ids, [(w3, table3)], emit_sum, tiles, koff)
        halo_sent(*halo3)

    halo_sent(*halo1)
    halo_sent(*halo2)


def local(feats, w_first, w_second, w_skip, send_tiles, send_counts, neighbours):
    ids, send_rows, counts = neighbours[0], send_tiles[0], send_counts[0]
    own = feats[0]
    tiles, channels, vox = own.shape
    dirs, cap = send_rows.shape
    table = pltpu.VMEM((tiles + dirs * cap + 1, channels, vox), own.dtype)
    weights = pltpu.VMEM(w_skip.shape, w_skip.dtype)
    box = pltpu.VMEM((dirs, cap, channels, vox), own.dtype)
    smem = pl.BlockSpec(memory_space=pltpu.SMEM)
    anywhere = pl.BlockSpec(memory_space=pl.ANY)
    second = pl.pallas_call(
        network,
        out_shape=jax.ShapeDtypeStruct((tiles, channels, vox), own.dtype),
        in_specs=[smem] * 3 + [anywhere] * 4,
        out_specs=pl.BlockSpec(memory_space=pltpu.VMEM),
        scratch_shapes=[table] * 3
        + [weights] * 3
        + [pltpu.VMEM((tiles // 2, channels, 2 * vox), jnp.float32)]
        + [box] * 6
        + [pltpu.SemaphoreType.DMA((4,))]
        + [pltpu.SemaphoreType.DMA((dirs,))] * 6
        + [pltpu.SemaphoreType.DMA((tiles // 2,))] * 2,
        compiler_params=pltpu.CompilerParams(
            collective_id=0, has_side_effects=True, vmem_limit_bytes=40 * 2**20
        ),
    )(ids, send_rows, counts, own, w_first[0], w_second[0], w_skip)
    return second[None]


def solution(mesh):
    placed = (
        P("section", "space", None, None),
        P("section", None, None, None),
        P("section", None, None, None),
        P(),
        P("section", "space", None),
        P("section", "space"),
        P("section", None, "space"),
    )
    return jax.shard_map(
        local,
        mesh=mesh,
        in_specs=placed,
        out_specs=P("section", "space", None, None),
        check_vma=False,
    )
```

```python
import jax
import jax.numpy as jnp
from jax import lax
from jax.experimental import pallas as pl
from jax.experimental.pallas import tpu as pltpu
from jax.sharding import PartitionSpec as P

GRID_B = 8

step_rows = (-1, -1, -1, 0, 0, 1, 1, 1)
step_cols = (-1, 0, 1, -1, 1, -1, 0, 1)


def conv_pair(ids, w, table, first, second):
    koff = w.shape[0]
    acc = None
    for i in range(0, koff, 2):
        lhs, rhs = [], []
        for k in range(i, min(i + 2, koff)):
            lhs.append(w[k])
            rhs.append(jnp.concatenate([table[ids[k, first]], table[ids[k, second]]], axis=1))
        part = jnp.dot(
            jnp.concatenate(lhs, axis=1),
            jnp.concatenate(rhs, axis=0),
            preferred_element_type=jnp.float32,
        )
        acc = part if acc is None else acc + part
    return acc


def conv_tiles(ids, w, table, emit, tiles):
    def body(step, _):
        emit(step * 2, conv_pair(ids, w, table, step * 2, step * 2 + 1))
        return 0

    lax.fori_loop(0, tiles // 2, body, 0)


MESH = pl.DeviceIdType.MESH


def network(
    ids, rows, counts, feats, w1_hbm, w2_hbm, w3_hbm, out,
    table1, table2, table3, w1, w2, w3, acc,
    outbox1, outbox2, outbox3, inbox1, inbox2, inbox3,
    local_sems, send1, recv1, send2, recv2, send3, recv3, send_skip, recv_skip,
):
    tiles, _, vox = feats.shape
    dirs, cap = rows.shape
    section = lax.axis_index("section")
    me = lax.axis_index("space")
    grid_a = lax.axis_size("space") // GRID_B
    row, col = me // GRID_B, me % GRID_B

    def inside(d, sign):
        r, c = row + sign * step_rows[d], col + sign * step_cols[d]
        return (r >= 0) & (r < grid_a) & (c >= 0) & (c < GRID_B)

    def target(d):
        return {"section": section, "space": me + step_rows[d] * GRID_B + step_cols[d]}

    sibling = {"section": 1 - section, "space": me}

    loads = [
        pltpu.make_async_copy(src, dst, local_sems.at[i])
        for i, (src, dst) in enumerate(
            [(feats, table1.at[pl.ds(0, tiles)]), (w1_hbm, w1), (w2_hbm, w2), (w3_hbm, w3)]
        )
    ]
    for load in loads:
        load.start()

    barrier = pltpu.get_barrier_semaphore()
    for d in range(dirs):

        @pl.when(inside(d, 1))
        def _():
            pl.semaphore_signal(barrier, inc=1, device_id=target(d), device_id_type=MESH)

    pl.semaphore_signal(barrier, inc=1, device_id=sibling, device_id_type=MESH)
    peers = jnp.int32(1)
    for d in range(dirs):
        peers += jnp.where(inside(d, -1), 1, 0).astype(jnp.int32)
    pl.semaphore_wait(barrier, peers)

    def halo_copy(d, outbox, inbox, send, recv):
        return pltpu.make_async_remote_copy(
            src_ref=outbox.at[d],
            dst_ref=inbox.at[d],
            send_sem=send.at[d],
            recv_sem=recv.at[d],
            device_id=target(d),
            device_id_type=MESH,
        )

    def halo_send(table, outbox, inbox, send, recv):
        for d in range(dirs):
            for j in range(cap):
                tile = table[rows[d, j]]
                outbox[d, j] = jnp.where(j < counts[d], tile, jnp.zeros_like(tile))

            @pl.when(inside(d, 1))
            def _():
                halo_copy(d, outbox, inbox, send, recv).start()

    def halo_receive(table, outbox, inbox, send, recv):
        for d in range(dirs):
            place = pl.ds(tiles + d * cap, cap)

            @pl.when(inside(d, -1))
            def _():
                halo_copy(d, outbox, inbox, send, recv).wait_recv()
                table[place] = inbox[d]

            @pl.when(jnp.logical_not(inside(d, -1)))
            def _():
                table[place] = jnp.zeros((cap,) + table.shape[1:], table.dtype)

        table[tiles + dirs * cap] = jnp.zeros(table.shape[1:], table.dtype)

    def halo_sent(outbox, inbox, send, recv):
        for d in range(dirs):

            @pl.when(inside(d, 1))
            def _():
                halo_copy(d, outbox, inbox, send, recv).wait_send()

    def skip_copy(t):
        return pltpu.make_async_remote_copy(
            src_ref=table2.at[pl.ds(t, 2)],
            dst_ref=table3.at[pl.ds(t, 2)],
            send_sem=send_skip.at[t // 2],
            recv_sem=recv_skip.at[t // 2],
            device_id=sibling,
            device_id_type=MESH,
        )

    halo1 = (outbox1, inbox1, send1, recv1)
    halo2 = (outbox2, inbox2, send2, recv2)
    halo3 = (outbox3, inbox3, send3, recv3)

    loads[0].wait()
    halo_send(table1, *halo1)
    halo_receive(table1, *halo1)
    loads[1].wait()

    def emit_first(t, part):
        part = jnp.maximum(part, 0.0).astype(table2.dtype)
        table2[t] = part[:, :vox]
        table2[t + 1] = part[:, vox:]

        @pl.when(section == 0)
        def _():
            skip_copy(t).start()

    def send_first(d, _):
        step = d + jnp.where(d >= dirs // 2, 1, 0).astype(jnp.int32)
        da, db = step // 3 - 1, step % 3 - 1
        r, c = row + da, col + db

        @pl.when((r >= 0) & (r < grid_a) & (c >= 0) & (c < GRID_B))
        def _():
            part = conv_pair(ids, w1, table1, rows[d, 0], rows[d, 1])
            part = jnp.maximum(part, 0.0).astype(outbox2.dtype)
            for j in range(cap):
                tile = part[:, j * vox : (j + 1) * vox]
                outbox2[d, j] = jnp.where(j < counts[d], tile, jnp.zeros_like(tile))
            pltpu.make_async_remote_copy(
                src_ref=outbox2.at[d],
                dst_ref=inbox2.at[d],
                send_sem=send2.at[d],
                recv_sem=recv2.at[d],
                device_id={"section": section, "space": me + da * GRID_B + db},
                device_id_type=MESH,
            ).start()

        return 0

    lax.fori_loop(0, dirs, send_first, 0)
    conv_tiles(ids, w1, table1, emit_first, tiles)

    @pl.when(section == 1)
    def _():
        lax.fori_loop(0, tiles // 2, lambda i, _: (skip_copy(2 * i).wait_recv(), 0)[1], 0)
        halo_send(table3, *halo3)

    halo_receive(table2, *halo2)
    loads[2].wait()
    loads[3].wait()

    def emit_out(t, part):
        acc[t // 2] = part
        part = jnp.maximum(part, 0.0).astype(out.dtype)
        out[t] = part[:, :vox]
        out[t + 1] = part[:, vox:]

    conv_tiles(ids, w2, table2, emit_out, tiles)

    @pl.when(section == 0)
    def _():
        lax.fori_loop(0, tiles // 2, lambda i, _: (skip_copy(2 * i).wait_send(), 0)[1], 0)

    @pl.when(section == 1)
    def _():
        halo_receive(table3, *halo3)

        def emit_sum(t, part):
            part = jnp.maximum(part + acc[t // 2], 0.0).astype(out.dtype)
            out[t] = part[:, :vox]
            out[t + 1] = part[:, vox:]

        conv_tiles(ids, w3, table3, emit_sum, tiles)
        halo_sent(*halo3)

    halo_sent(*halo1)
    halo_sent(*halo2)


def local(feats, w_first, w_second, w_skip, send_tiles, send_counts, neighbours):
    ids, send_rows, counts = neighbours[0], send_tiles[0], send_counts[0]
    own = feats[0]
    tiles, channels, vox = own.shape
    dirs, cap = send_rows.shape
    table = pltpu.VMEM((tiles + dirs * cap + 1, channels, vox), own.dtype)
    weights = pltpu.VMEM(w_skip.shape, w_skip.dtype)
    box = pltpu.VMEM((dirs, cap, channels, vox), own.dtype)
    smem = pl.BlockSpec(memory_space=pltpu.SMEM)
    anywhere = pl.BlockSpec(memory_space=pl.ANY)
    second = pl.pallas_call(
        network,
        out_shape=jax.ShapeDtypeStruct((tiles, channels, vox), own.dtype),
        in_specs=[smem] * 3 + [anywhere] * 4,
        out_specs=pl.BlockSpec(memory_space=pltpu.VMEM),
        scratch_shapes=[table] * 3
        + [weights] * 3
        + [pltpu.VMEM((tiles // 2, channels, 2 * vox), jnp.float32)]
        + [box] * 6
        + [pltpu.SemaphoreType.DMA((4,))]
        + [pltpu.SemaphoreType.DMA((dirs,))] * 6
        + [pltpu.SemaphoreType.DMA((tiles // 2,))] * 2,
        compiler_params=pltpu.CompilerParams(
            collective_id=0, has_side_effects=True, vmem_limit_bytes=40 * 2**20
        ),
    )(ids, send_rows, counts, own, w_first[0], w_second[0], w_skip)
    return second[None]


def solution(mesh):
    placed = (
        P("section", "space", None, None),
        P("section", None, None, None),
        P("section", None, None, None),
        P(),
        P("section", "space", None),
        P("section", "space"),
        P("section", None, "space"),
    )
    return jax.shard_map(
        local,
        mesh=mesh,
        in_specs=placed,
        out_specs=P("section", "space", None, None),
        check_vma=False,
    )
```

```python
import jax
import jax.numpy as jnp
from jax import lax
from jax.experimental import pallas as pl
from jax.experimental.pallas import tpu as pltpu
from jax.sharding import PartitionSpec as P

GRID_B = 8

step_rows = (-1, -1, -1, 0, 0, 1, 1, 1)
step_cols = (-1, 0, 1, -1, 1, -1, 0, 1)


def conv_pair(ids, w, table, first, second):
    koff = w.shape[0]
    acc = None
    for i in range(0, koff, 2):
        lhs, rhs = [], []
        for k in range(i, min(i + 2, koff)):
            lhs.append(w[k])
            rhs.append(jnp.concatenate([table[ids[first, k]], table[ids[second, k]]], axis=1))
        part = jnp.dot(
            jnp.concatenate(lhs, axis=1),
            jnp.concatenate(rhs, axis=0),
            preferred_element_type=jnp.float32,
        )
        acc = part if acc is None else acc + part
    return acc


def conv_tiles(ids, w, table, emit, tiles):
    def body(step, _):
        emit(step * 2, conv_pair(ids, w, table, step * 2, step * 2 + 1))
        return 0

    lax.fori_loop(0, tiles // 2, body, 0)


MESH = pl.DeviceIdType.MESH


def network(
    ids, rows, counts, feats, w1_hbm, w2_hbm, w3_hbm, out,
    table1, table2, table3, w1, w2, w3, acc,
    outbox1, outbox2, outbox3, inbox1, inbox2, inbox3,
    local_sems, send1, recv1, send2, recv2, send3, recv3, send_skip, recv_skip,
):
    tiles, _, vox = feats.shape
    cap, dirs = rows.shape
    section = lax.axis_index("section")
    me = lax.axis_index("space")
    grid_a = lax.axis_size("space") // GRID_B
    row, col = me // GRID_B, me % GRID_B

    def inside(d, sign):
        r, c = row + sign * step_rows[d], col + sign * step_cols[d]
        return (r >= 0) & (r < grid_a) & (c >= 0) & (c < GRID_B)

    def target(d):
        return {"section": section, "space": me + step_rows[d] * GRID_B + step_cols[d]}

    sibling = {"section": 1 - section, "space": me}

    loads = [
        pltpu.make_async_copy(src, dst, local_sems.at[i])
        for i, (src, dst) in enumerate(
            [(feats, table1.at[pl.ds(0, tiles)]), (w1_hbm, w1), (w2_hbm, w2), (w3_hbm, w3)]
        )
    ]
    for load in loads:
        load.start()

    barrier = pltpu.get_barrier_semaphore()
    for d in range(dirs):

        @pl.when(inside(d, 1))
        def _():
            pl.semaphore_signal(barrier, inc=1, device_id=target(d), device_id_type=MESH)

    pl.semaphore_signal(barrier, inc=1, device_id=sibling, device_id_type=MESH)
    peers = jnp.int32(1)
    for d in range(dirs):
        peers += jnp.where(inside(d, -1), 1, 0).astype(jnp.int32)
    pl.semaphore_wait(barrier, peers)

    def halo_copy(d, outbox, inbox, send, recv):
        return pltpu.make_async_remote_copy(
            src_ref=outbox.at[d],
            dst_ref=inbox.at[d],
            send_sem=send.at[d],
            recv_sem=recv.at[d],
            device_id=target(d),
            device_id_type=MESH,
        )

    def halo_send(table, outbox, inbox, send, recv):
        for d in range(dirs):
            for j in range(cap):
                tile = table[rows[j, d]]
                outbox[d, j] = jnp.where(j < counts[d], tile, jnp.zeros_like(tile))

            @pl.when(inside(d, 1))
            def _():
                halo_copy(d, outbox, inbox, send, recv).start()

    def halo_receive(table, outbox, inbox, send, recv):
        for d in range(dirs):
            place = pl.ds(tiles + d * cap, cap)

            @pl.when(inside(d, -1))
            def _():
                halo_copy(d, outbox, inbox, send, recv).wait_recv()
                table[place] = inbox[d]

            @pl.when(jnp.logical_not(inside(d, -1)))
            def _():
                table[place] = jnp.zeros((cap,) + table.shape[1:], table.dtype)

        table[tiles + dirs * cap] = jnp.zeros(table.shape[1:], table.dtype)

    def halo_sent(outbox, inbox, send, recv):
        for d in range(dirs):

            @pl.when(inside(d, 1))
            def _():
                halo_copy(d, outbox, inbox, send, recv).wait_send()

    def skip_copy(t):
        return pltpu.make_async_remote_copy(
            src_ref=table2.at[pl.ds(t, 2)],
            dst_ref=table3.at[pl.ds(t, 2)],
            send_sem=send_skip.at[t // 2],
            recv_sem=recv_skip.at[t // 2],
            device_id=sibling,
            device_id_type=MESH,
        )

    halo1 = (outbox1, inbox1, send1, recv1)
    halo2 = (outbox2, inbox2, send2, recv2)
    halo3 = (outbox3, inbox3, send3, recv3)

    loads[0].wait()
    halo_send(table1, *halo1)
    halo_receive(table1, *halo1)
    loads[1].wait()

    def emit_first(t, part):
        part = jnp.maximum(part, 0.0).astype(table2.dtype)
        table2[t] = part[:, :vox]
        table2[t + 1] = part[:, vox:]

        @pl.when(section == 0)
        def _():
            skip_copy(t).start()

    def send_first(d, _):
        step = d + jnp.where(d >= dirs // 2, 1, 0).astype(jnp.int32)
        da, db = step // 3 - 1, step % 3 - 1
        r, c = row + da, col + db

        @pl.when((r >= 0) & (r < grid_a) & (c >= 0) & (c < GRID_B))
        def _():
            part = conv_pair(ids, w1, table1, rows[0, d], rows[1, d])
            part = jnp.maximum(part, 0.0).astype(outbox2.dtype)
            for j in range(cap):
                tile = part[:, j * vox : (j + 1) * vox]
                outbox2[d, j] = jnp.where(j < counts[d], tile, jnp.zeros_like(tile))
            pltpu.make_async_remote_copy(
                src_ref=outbox2.at[d],
                dst_ref=inbox2.at[d],
                send_sem=send2.at[d],
                recv_sem=recv2.at[d],
                device_id={"section": section, "space": me + da * GRID_B + db},
                device_id_type=MESH,
            ).start()

        return 0

    lax.fori_loop(0, dirs, send_first, 0)
    conv_tiles(ids, w1, table1, emit_first, tiles)

    @pl.when(section == 1)
    def _():
        lax.fori_loop(0, tiles // 2, lambda i, _: (skip_copy(2 * i).wait_recv(), 0)[1], 0)
        halo_send(table3, *halo3)

    halo_receive(table2, *halo2)
    loads[2].wait()
    loads[3].wait()

    def emit_out(t, part):
        acc[t // 2] = part
        part = jnp.maximum(part, 0.0).astype(out.dtype)
        out[t] = part[:, :vox]
        out[t + 1] = part[:, vox:]

    conv_tiles(ids, w2, table2, emit_out, tiles)

    @pl.when(section == 0)
    def _():
        lax.fori_loop(0, tiles // 2, lambda i, _: (skip_copy(2 * i).wait_send(), 0)[1], 0)

    @pl.when(section == 1)
    def _():
        halo_receive(table3, *halo3)

        def emit_sum(t, part):
            part = jnp.maximum(part + acc[t // 2], 0.0).astype(out.dtype)
            out[t] = part[:, :vox]
            out[t + 1] = part[:, vox:]

        conv_tiles(ids, w3, table3, emit_sum, tiles)
        halo_sent(*halo3)

    halo_sent(*halo1)
    halo_sent(*halo2)


def local(feats, w_first, w_second, w_skip, send_tiles, send_counts, neighbours):
    ids, send_rows, counts = neighbours[0], send_tiles[0], send_counts[0]
    own = feats[0]
    tiles, channels, vox = own.shape
    dirs, cap = send_rows.shape
    table = pltpu.VMEM((tiles + dirs * cap + 1, channels, vox), own.dtype)
    weights = pltpu.VMEM(w_skip.shape, w_skip.dtype)
    box = pltpu.VMEM((dirs, cap, channels, vox), own.dtype)
    smem = pl.BlockSpec(memory_space=pltpu.SMEM)
    anywhere = pl.BlockSpec(memory_space=pltpu.HBM)
    second = pl.pallas_call(
        network,
        out_shape=jax.ShapeDtypeStruct((tiles, channels, vox), own.dtype),
        in_specs=[smem] * 3 + [anywhere] * 4,
        out_specs=pl.BlockSpec(memory_space=pltpu.VMEM),
        scratch_shapes=[table] * 3
        + [weights] * 3
        + [pltpu.VMEM((tiles // 2, channels, 2 * vox), jnp.float32)]
        + [box] * 6
        + [pltpu.SemaphoreType.DMA((4,))]
        + [pltpu.SemaphoreType.DMA((dirs,))] * 6
        + [pltpu.SemaphoreType.DMA((tiles // 2,))] * 2,
        compiler_params=pltpu.CompilerParams(
            collective_id=0, has_side_effects=True, vmem_limit_bytes=56 * 2**20
        ),
    )(ids.T, send_rows.T, counts, own, w_first[0], w_second[0], w_skip)
    return second[None]


def solution(mesh):
    placed = (
        P("section", "space", None, None),
        P("section", None, None, None),
        P("section", None, None, None),
        P(),
        P("section", "space", None),
        P("section", "space"),
        P("section", None, "space"),
    )
    return jax.shard_map(
        local,
        mesh=mesh,
        in_specs=placed,
        out_specs=P("section", "space", None, None),
        check_vma=False,
    )
```

```python
import jax
import jax.numpy as jnp
from jax import lax
from jax.experimental import pallas as pl
from jax.experimental.pallas import tpu as pltpu
from jax.sharding import PartitionSpec as P

GRID_B = 8

step_rows = (-1, -1, -1, 0, 0, 1, 1, 1)
step_cols = (-1, 0, 1, -1, 1, -1, 0, 1)


def conv_pair(ids, w, table, first, second):
    koff = w.shape[0]
    acc = None
    for i in range(0, koff, 2):
        lhs, rhs = [], []
        for k in range(i, min(i + 2, koff)):
            lhs.append(w[k])
            rhs.append(jnp.concatenate([table[ids[first, k]], table[ids[second, k]]], axis=1))
        part = jnp.dot(
            jnp.concatenate(lhs, axis=1),
            jnp.concatenate(rhs, axis=0),
            preferred_element_type=jnp.float32,
        )
        acc = part if acc is None else acc + part
    return acc


def conv_tiles(ids, w, table, emit, tiles):
    width = 4 if tiles % 4 == 0 else 2

    def body(step, _):
        firsts = [step * width + i for i in range(0, width, 2)]
        parts = [conv_pair(ids, w, table, t, t + 1) for t in firsts]
        for t, part in zip(firsts, parts):
            emit(t, part)
        return 0

    lax.fori_loop(0, tiles // width, body, 0)


MESH = pl.DeviceIdType.MESH


def network(
    ids, rows, counts, feats, w1_hbm, w2_hbm, w3_hbm, out,
    table1, table2, table3, w1, w2, w3, acc,
    outbox1, outbox2, outbox3, inbox1, inbox2, inbox3,
    local_sems, send1, recv1, send2, recv2, send3, recv3, send_skip, recv_skip,
):
    tiles, _, vox = feats.shape
    cap, dirs = rows.shape
    section = lax.axis_index("section")
    me = lax.axis_index("space")
    grid_a = lax.axis_size("space") // GRID_B
    row, col = me // GRID_B, me % GRID_B

    def inside(d, sign):
        r, c = row + sign * step_rows[d], col + sign * step_cols[d]
        return (r >= 0) & (r < grid_a) & (c >= 0) & (c < GRID_B)

    def target(d):
        return {"section": section, "space": me + step_rows[d] * GRID_B + step_cols[d]}

    sibling = {"section": 1 - section, "space": me}

    loads = [
        pltpu.make_async_copy(src, dst, local_sems.at[i])
        for i, (src, dst) in enumerate(
            [(feats, table1.at[pl.ds(0, tiles)]), (w1_hbm, w1), (w2_hbm, w2), (w3_hbm, w3)]
        )
    ]
    for load in loads:
        load.start()

    barrier = pltpu.get_barrier_semaphore()
    for d in range(dirs):

        @pl.when(inside(d, 1))
        def _():
            pl.semaphore_signal(barrier, inc=1, device_id=target(d), device_id_type=MESH)

    pl.semaphore_signal(barrier, inc=1, device_id=sibling, device_id_type=MESH)
    peers = jnp.int32(1)
    for d in range(dirs):
        peers += jnp.where(inside(d, -1), 1, 0).astype(jnp.int32)
    pl.semaphore_wait(barrier, peers)

    def halo_copy(d, outbox, inbox, send, recv):
        return pltpu.make_async_remote_copy(
            src_ref=outbox.at[d],
            dst_ref=inbox.at[d],
            send_sem=send.at[d],
            recv_sem=recv.at[d],
            device_id=target(d),
            device_id_type=MESH,
        )

    def halo_send(table, outbox, inbox, send, recv):
        for d in sorted(range(dirs), key=lambda d: step_rows[d] == 0):
            for j in range(cap):
                tile = table[rows[j, d]]
                outbox[d, j] = jnp.where(j < counts[d], tile, jnp.zeros_like(tile))

            @pl.when(inside(d, 1))
            def _():
                halo_copy(d, outbox, inbox, send, recv).start()

    def halo_receive(table, outbox, inbox, send, recv):
        for d in range(dirs):
            place = pl.ds(tiles + d * cap, cap)

            @pl.when(inside(d, -1))
            def _():
                halo_copy(d, outbox, inbox, send, recv).wait_recv()
                table[place] = inbox[d]

            @pl.when(jnp.logical_not(inside(d, -1)))
            def _():
                table[place] = jnp.zeros((cap,) + table.shape[1:], table.dtype)

        table[tiles + dirs * cap] = jnp.zeros(table.shape[1:], table.dtype)

    def halo_sent(outbox, inbox, send, recv):
        for d in range(dirs):

            @pl.when(inside(d, 1))
            def _():
                halo_copy(d, outbox, inbox, send, recv).wait_send()

    def skip_copy(t):
        return pltpu.make_async_remote_copy(
            src_ref=table2.at[pl.ds(t, 2)],
            dst_ref=table3.at[pl.ds(t, 2)],
            send_sem=send_skip.at[t // 2],
            recv_sem=recv_skip.at[t // 2],
            device_id=sibling,
            device_id_type=MESH,
        )

    halo1 = (outbox1, inbox1, send1, recv1)
    halo2 = (outbox2, inbox2, send2, recv2)
    halo3 = (outbox3, inbox3, send3, recv3)

    loads[0].wait()
    halo_send(table1, *halo1)
    halo_receive(table1, *halo1)
    loads[1].wait()

    def emit_first(t, part):
        part = jnp.maximum(part, 0.0).astype(table2.dtype)
        table2[t] = part[:, :vox]
        table2[t + 1] = part[:, vox:]

        @pl.when(section == 0)
        def _():
            skip_copy(t).start()

    def send_first(d, _):
        step = d + jnp.where(d >= dirs // 2, 1, 0).astype(jnp.int32)
        da, db = step // 3 - 1, step % 3 - 1
        r, c = row + da, col + db

        @pl.when((r >= 0) & (r < grid_a) & (c >= 0) & (c < GRID_B))
        def _():
            part = conv_pair(ids, w1, table1, rows[0, d], rows[1, d])
            part = jnp.maximum(part, 0.0).astype(outbox2.dtype)
            for j in range(cap):
                tile = part[:, j * vox : (j + 1) * vox]
                outbox2[d, j] = jnp.where(j < counts[d], tile, jnp.zeros_like(tile))
            pltpu.make_async_remote_copy(
                src_ref=outbox2.at[d],
                dst_ref=inbox2.at[d],
                send_sem=send2.at[d],
                recv_sem=recv2.at[d],
                device_id={"section": section, "space": me + da * GRID_B + db},
                device_id_type=MESH,
            ).start()

        return 0

    lax.fori_loop(0, dirs, send_first, 0)
    conv_tiles(ids, w1, table1, emit_first, tiles)

    @pl.when(section == 1)
    def _():
        lax.fori_loop(0, tiles // 2, lambda i, _: (skip_copy(2 * i).wait_recv(), 0)[1], 0)
        halo_send(table3, *halo3)

    halo_receive(table2, *halo2)
    loads[2].wait()
    loads[3].wait()

    def emit_out(t, part):
        acc[t // 2] = part
        part = jnp.maximum(part, 0.0).astype(out.dtype)
        out[t] = part[:, :vox]
        out[t + 1] = part[:, vox:]

    conv_tiles(ids, w2, table2, emit_out, tiles)

    @pl.when(section == 0)
    def _():
        lax.fori_loop(0, tiles // 2, lambda i, _: (skip_copy(2 * i).wait_send(), 0)[1], 0)

    @pl.when(section == 1)
    def _():
        halo_receive(table3, *halo3)

        def emit_sum(t, part):
            part = jnp.maximum(part + acc[t // 2], 0.0).astype(out.dtype)
            out[t] = part[:, :vox]
            out[t + 1] = part[:, vox:]

        conv_tiles(ids, w3, table3, emit_sum, tiles)
        halo_sent(*halo3)

    halo_sent(*halo1)
    halo_sent(*halo2)


def local(feats, w_first, w_second, w_skip, send_tiles, send_counts, neighbours):
    ids, send_rows, counts = neighbours[0], send_tiles[0], send_counts[0]
    own = feats[0]
    tiles, channels, vox = own.shape
    dirs, cap = send_rows.shape
    table = pltpu.VMEM((tiles + dirs * cap + 1, channels, vox), own.dtype)
    weights = pltpu.VMEM(w_skip.shape, w_skip.dtype)
    box = pltpu.VMEM((dirs, cap, channels, vox), own.dtype)
    smem = pl.BlockSpec(memory_space=pltpu.SMEM)
    anywhere = pl.BlockSpec(memory_space=pltpu.HBM)
    second = pl.pallas_call(
        network,
        out_shape=jax.ShapeDtypeStruct((tiles, channels, vox), own.dtype),
        in_specs=[smem] * 3 + [anywhere] * 4,
        out_specs=pl.BlockSpec(memory_space=pltpu.VMEM),
        scratch_shapes=[table] * 3
        + [weights] * 3
        + [pltpu.VMEM((tiles // 2, channels, 2 * vox), jnp.float32)]
        + [box] * 6
        + [pltpu.SemaphoreType.DMA((4,))]
        + [pltpu.SemaphoreType.DMA((dirs,))] * 6
        + [pltpu.SemaphoreType.DMA((tiles // 2,))] * 2,
        compiler_params=pltpu.CompilerParams(
            collective_id=0, has_side_effects=True, vmem_limit_bytes=56 * 2**20
        ),
    )(ids.T, send_rows.T, counts, own, w_first[0], w_second[0], w_skip)
    return second[None]


def solution(mesh):
    placed = (
        P("section", "space", None, None),
        P("section", None, None, None),
        P("section", None, None, None),
        P(),
        P("section", "space", None),
        P("section", "space"),
        P("section", None, "space"),
    )
    return jax.shard_map(
        local,
        mesh=mesh,
        in_specs=placed,
        out_specs=P("section", "space", None, None),
        check_vma=False,
    )
```

```python
import jax
import jax.numpy as jnp
from jax import lax
from jax.experimental import pallas as pl
from jax.experimental.pallas import tpu as pltpu
from jax.sharding import PartitionSpec as P

GRID_B = 8

step_rows = (-1, -1, -1, 0, 0, 1, 1, 1)
step_cols = (-1, 0, 1, -1, 1, -1, 0, 1)


def conv_pair(ids, w, table, first, second):
    koff = w.shape[0]
    acc = None
    for i in range(0, koff, 2):
        lhs, rhs = [], []
        for k in range(i, min(i + 2, koff)):
            lhs.append(w[k])
            rhs.append(jnp.concatenate([table[ids[first, k]], table[ids[second, k]]], axis=1))
        part = jnp.dot(
            jnp.concatenate(lhs, axis=1),
            jnp.concatenate(rhs, axis=0),
            preferred_element_type=jnp.float32,
        )
        acc = part if acc is None else acc + part
    return acc


def conv_tiles(ids, w, table, emit, tiles):
    width = 4 if tiles % 4 == 0 else 2

    def body(step, _):
        firsts = [step * width + i for i in range(0, width, 2)]
        parts = [conv_pair(ids, w, table, t, t + 1) for t in firsts]
        for t, part in zip(firsts, parts):
            emit(t, part)
        return 0

    lax.fori_loop(0, tiles // width, body, 0)


MESH = pl.DeviceIdType.MESH


def network(
    ids, rows, counts, feats, w1_hbm, w2_hbm, w3_hbm, out,
    table1, table2, table3, w1, w2, w3, acc,
    outbox1, outbox2, outbox3, inbox1, inbox2, inbox3,
    local_sems, send1, recv1, send2, recv2, send3, recv3, send_skip, recv_skip,
):
    tiles, _, vox = feats.shape
    cap, dirs = rows.shape
    section = lax.axis_index("section")
    me = lax.axis_index("space")
    grid_a = lax.axis_size("space") // GRID_B
    row, col = me // GRID_B, me % GRID_B

    def inside(d, sign):
        r, c = row + sign * step_rows[d], col + sign * step_cols[d]
        return (r >= 0) & (r < grid_a) & (c >= 0) & (c < GRID_B)

    def target(d):
        return {"section": section, "space": me + step_rows[d] * GRID_B + step_cols[d]}

    sibling = {"section": 1 - section, "space": me}

    loads = [
        pltpu.make_async_copy(src, dst, local_sems.at[i])
        for i, (src, dst) in enumerate(
            [(feats, table1.at[pl.ds(0, tiles)]), (w1_hbm, w1), (w2_hbm, w2), (w3_hbm, w3)]
        )
    ]
    for load in loads:
        load.start()

    barrier = pltpu.get_barrier_semaphore()
    for d in range(dirs):

        @pl.when(inside(d, 1))
        def _():
            pl.semaphore_signal(barrier, inc=1, device_id=target(d), device_id_type=MESH)

    pl.semaphore_signal(barrier, inc=1, device_id=sibling, device_id_type=MESH)
    peers = jnp.int32(1)
    for d in range(dirs):
        peers += jnp.where(inside(d, -1), 1, 0).astype(jnp.int32)
    pl.semaphore_wait(barrier, peers)

    def halo_copy(d, outbox, inbox, send, recv):
        return pltpu.make_async_remote_copy(
            src_ref=outbox.at[d],
            dst_ref=inbox.at[d],
            send_sem=send.at[d],
            recv_sem=recv.at[d],
            device_id=target(d),
            device_id_type=MESH,
        )

    def halo_send(table, outbox, inbox, send, recv):
        for d in sorted(range(dirs), key=lambda d: step_rows[d] == 0):
            for j in range(cap):
                tile = table[rows[j, d]]
                outbox[d, j] = jnp.where(j < counts[d], tile, jnp.zeros_like(tile))

            @pl.when(inside(d, 1))
            def _():
                halo_copy(d, outbox, inbox, send, recv).start()

    def halo_receive(table, outbox, inbox, send, recv):
        for d in range(dirs):
            place = pl.ds(tiles + d * cap, cap)

            @pl.when(inside(d, -1))
            def _():
                halo_copy(d, outbox, inbox, send, recv).wait_recv()
                table[place] = inbox[d]

            @pl.when(jnp.logical_not(inside(d, -1)))
            def _():
                table[place] = jnp.zeros((cap,) + table.shape[1:], table.dtype)

        table[tiles + dirs * cap] = jnp.zeros(table.shape[1:], table.dtype)

    def halo_sent(outbox, inbox, send, recv):
        for d in range(dirs):

            @pl.when(inside(d, 1))
            def _():
                halo_copy(d, outbox, inbox, send, recv).wait_send()

    def skip_copy(t):
        return pltpu.make_async_remote_copy(
            src_ref=table2.at[pl.ds(t, 2)],
            dst_ref=table3.at[pl.ds(t, 2)],
            send_sem=send_skip.at[t // 2],
            recv_sem=recv_skip.at[t // 2],
            device_id=sibling,
            device_id_type=MESH,
        )

    halo1 = (outbox1, inbox1, send1, recv1)
    halo2 = (outbox2, inbox2, send2, recv2)
    halo3 = (outbox3, inbox3, send3, recv3)

    loads[0].wait()
    halo_send(table1, *halo1)
    halo_receive(table1, *halo1)
    loads[1].wait()

    def emit_first(t, part):
        part = jnp.maximum(part, 0.0).astype(table2.dtype)
        table2[t] = part[:, :vox]
        table2[t + 1] = part[:, vox:]

        @pl.when(section == 0)
        def _():
            skip_copy(t).start()

    def send_first(d, _):
        step = d + jnp.where(d >= dirs // 2, 1, 0).astype(jnp.int32)
        da, db = step // 3 - 1, step % 3 - 1
        r, c = row + da, col + db

        @pl.when((r >= 0) & (r < grid_a) & (c >= 0) & (c < GRID_B))
        def _():
            part = conv_pair(ids, w1, table1, rows[0, d], rows[1, d])
            part = jnp.maximum(part, 0.0).astype(outbox2.dtype)
            for j in range(cap):
                tile = part[:, j * vox : (j + 1) * vox]
                outbox2[d, j] = jnp.where(j < counts[d], tile, jnp.zeros_like(tile))
            pltpu.make_async_remote_copy(
                src_ref=outbox2.at[d],
                dst_ref=inbox2.at[d],
                send_sem=send2.at[d],
                recv_sem=recv2.at[d],
                device_id={"section": section, "space": me + da * GRID_B + db},
                device_id_type=MESH,
            ).start()

        return 0

    @pl.when(section == 1)
    def _():
        lax.fori_loop(0, dirs, send_first, 0)

    conv_tiles(ids, w1, table1, emit_first, tiles)

    @pl.when(section == 0)
    def _():
        lax.fori_loop(0, dirs, send_first, 0)

    @pl.when(section == 1)
    def _():
        lax.fori_loop(0, tiles // 2, lambda i, _: (skip_copy(2 * i).wait_recv(), 0)[1], 0)
        halo_send(table3, *halo3)

    halo_receive(table2, *halo2)
    loads[2].wait()
    loads[3].wait()

    def emit_out(t, part):
        acc[t // 2] = part
        part = jnp.maximum(part, 0.0).astype(out.dtype)
        out[t] = part[:, :vox]
        out[t + 1] = part[:, vox:]

    conv_tiles(ids, w2, table2, emit_out, tiles)

    @pl.when(section == 0)
    def _():
        lax.fori_loop(0, tiles // 2, lambda i, _: (skip_copy(2 * i).wait_send(), 0)[1], 0)

    @pl.when(section == 1)
    def _():
        halo_receive(table3, *halo3)

        def emit_sum(t, part):
            part = jnp.maximum(part + acc[t // 2], 0.0).astype(out.dtype)
            out[t] = part[:, :vox]
            out[t + 1] = part[:, vox:]

        conv_tiles(ids, w3, table3, emit_sum, tiles)
        halo_sent(*halo3)

    halo_sent(*halo1)
    halo_sent(*halo2)


def local(feats, w_first, w_second, w_skip, send_tiles, send_counts, neighbours):
    ids, send_rows, counts = neighbours[0], send_tiles[0], send_counts[0]
    own = feats[0]
    tiles, channels, vox = own.shape
    dirs, cap = send_rows.shape
    table = pltpu.VMEM((tiles + dirs * cap + 1, channels, vox), own.dtype)
    weights = pltpu.VMEM(w_skip.shape, w_skip.dtype)
    box = pltpu.VMEM((dirs, cap, channels, vox), own.dtype)
    smem = pl.BlockSpec(memory_space=pltpu.SMEM)
    anywhere = pl.BlockSpec(memory_space=pltpu.HBM)
    second = pl.pallas_call(
        network,
        out_shape=jax.ShapeDtypeStruct((tiles, channels, vox), own.dtype),
        in_specs=[smem] * 3 + [anywhere] * 4,
        out_specs=pl.BlockSpec(memory_space=pltpu.VMEM),
        scratch_shapes=[table] * 3
        + [weights] * 3
        + [pltpu.VMEM((tiles // 2, channels, 2 * vox), jnp.float32)]
        + [box] * 6
        + [pltpu.SemaphoreType.DMA((4,))]
        + [pltpu.SemaphoreType.DMA((dirs,))] * 6
        + [pltpu.SemaphoreType.DMA((tiles // 2,))] * 2,
        compiler_params=pltpu.CompilerParams(
            collective_id=0, has_side_effects=True, vmem_limit_bytes=56 * 2**20
        ),
    )(ids.T, send_rows.T, counts, own, w_first[0], w_second[0], w_skip)
    return second[None]


def solution(mesh):
    placed = (
        P("section", "space", None, None),
        P("section", None, None, None),
        P("section", None, None, None),
        P(),
        P("section", "space", None),
        P("section", "space"),
        P("section", None, "space"),
    )
    return jax.shard_map(
        local,
        mesh=mesh,
        in_specs=placed,
        out_specs=P("section", "space", None, None),
        check_vma=False,
    )
```

```python
import jax
import jax.numpy as jnp
from jax import lax
from jax.experimental import pallas as pl
from jax.experimental.pallas import tpu as pltpu
from jax.sharding import PartitionSpec as P

GRID_B = 8

step_rows = (-1, -1, -1, 0, 0, 1, 1, 1)
step_cols = (-1, 0, 1, -1, 1, -1, 0, 1)


def conv_pair(ids, w, table, first, second):
    koff = w.shape[0]
    acc = None
    for i in range(0, koff, 2):
        lhs, rhs = [], []
        for k in range(i, min(i + 2, koff)):
            lhs.append(w[k])
            rhs.append(jnp.concatenate([table[ids[first, k]], table[ids[second, k]]], axis=1))
        part = jnp.dot(
            jnp.concatenate(lhs, axis=1),
            jnp.concatenate(rhs, axis=0),
            preferred_element_type=jnp.float32,
        )
        acc = part if acc is None else acc + part
    return acc


def conv_tiles(ids, w, table, emit, tiles):
    width = 8 if tiles % 8 == 0 else 2

    def body(step, _):
        firsts = [step * width + i for i in range(0, width, 2)]
        parts = [conv_pair(ids, w, table, t, t + 1) for t in firsts]
        for t, part in zip(firsts, parts):
            emit(t, part)
        return 0

    lax.fori_loop(0, tiles // width, body, 0)


MESH = pl.DeviceIdType.MESH


def network(
    ids, rows, counts, feats, w1_hbm, w2_hbm, w3_hbm, out,
    table1, table2, table3, w1, w2, w3, acc,
    outbox1, outbox2, outbox3, inbox1, inbox2, inbox3,
    local_sems, send1, recv1, send2, recv2, send3, recv3, send_skip, recv_skip,
):
    tiles, _, vox = feats.shape
    cap, dirs = rows.shape
    section = lax.axis_index("section")
    me = lax.axis_index("space")
    grid_a = lax.axis_size("space") // GRID_B
    row, col = me // GRID_B, me % GRID_B

    def inside(d, sign):
        r, c = row + sign * step_rows[d], col + sign * step_cols[d]
        return (r >= 0) & (r < grid_a) & (c >= 0) & (c < GRID_B)

    def target(d):
        return {"section": section, "space": me + step_rows[d] * GRID_B + step_cols[d]}

    sibling = {"section": 1 - section, "space": me}

    loads = [
        pltpu.make_async_copy(src, dst, local_sems.at[i])
        for i, (src, dst) in enumerate(
            [(feats, table1.at[pl.ds(0, tiles)]), (w1_hbm, w1), (w2_hbm, w2), (w3_hbm, w3)]
        )
    ]
    for load in loads:
        load.start()

    barrier = pltpu.get_barrier_semaphore()
    for d in range(dirs):

        @pl.when(inside(d, 1))
        def _():
            pl.semaphore_signal(barrier, inc=1, device_id=target(d), device_id_type=MESH)

    pl.semaphore_signal(barrier, inc=1, device_id=sibling, device_id_type=MESH)
    peers = jnp.int32(1)
    for d in range(dirs):
        peers += jnp.where(inside(d, -1), 1, 0).astype(jnp.int32)
    pl.semaphore_wait(barrier, peers)

    def halo_copy(d, outbox, inbox, send, recv):
        return pltpu.make_async_remote_copy(
            src_ref=outbox.at[d],
            dst_ref=inbox.at[d],
            send_sem=send.at[d],
            recv_sem=recv.at[d],
            device_id=target(d),
            device_id_type=MESH,
        )

    def halo_send(table, outbox, inbox, send, recv):
        for d in sorted(range(dirs), key=lambda d: step_rows[d] == 0):
            for j in range(cap):
                tile = table[rows[j, d]]
                outbox[d, j] = jnp.where(j < counts[d], tile, jnp.zeros_like(tile))

            @pl.when(inside(d, 1))
            def _():
                halo_copy(d, outbox, inbox, send, recv).start()

    def halo_receive(table, outbox, inbox, send, recv):
        for d in range(dirs):
            place = pl.ds(tiles + d * cap, cap)

            @pl.when(inside(d, -1))
            def _():
                halo_copy(d, outbox, inbox, send, recv).wait_recv()
                table[place] = inbox[d]

            @pl.when(jnp.logical_not(inside(d, -1)))
            def _():
                table[place] = jnp.zeros((cap,) + table.shape[1:], table.dtype)

        table[tiles + dirs * cap] = jnp.zeros(table.shape[1:], table.dtype)

    def halo_sent(outbox, inbox, send, recv):
        for d in range(dirs):

            @pl.when(inside(d, 1))
            def _():
                halo_copy(d, outbox, inbox, send, recv).wait_send()

    def skip_copy(t):
        return pltpu.make_async_remote_copy(
            src_ref=table2.at[pl.ds(t, 2)],
            dst_ref=table3.at[pl.ds(t, 2)],
            send_sem=send_skip.at[t // 2],
            recv_sem=recv_skip.at[t // 2],
            device_id=sibling,
            device_id_type=MESH,
        )

    halo1 = (outbox1, inbox1, send1, recv1)
    halo2 = (outbox2, inbox2, send2, recv2)
    halo3 = (outbox3, inbox3, send3, recv3)

    loads[0].wait()
    halo_send(table1, *halo1)
    halo_receive(table1, *halo1)
    loads[1].wait()

    def emit_first(t, part):
        part = jnp.maximum(part, 0.0).astype(table2.dtype)
        table2[t] = part[:, :vox]
        table2[t + 1] = part[:, vox:]

        @pl.when(section == 0)
        def _():
            skip_copy(t).start()

    def send_first(d, _):
        step = d + jnp.where(d >= dirs // 2, 1, 0).astype(jnp.int32)
        da, db = step // 3 - 1, step % 3 - 1
        r, c = row + da, col + db

        @pl.when((r >= 0) & (r < grid_a) & (c >= 0) & (c < GRID_B))
        def _():
            part = conv_pair(ids, w1, table1, rows[0, d], rows[1, d])
            part = jnp.maximum(part, 0.0).astype(outbox2.dtype)
            for j in range(cap):
                tile = part[:, j * vox : (j + 1) * vox]
                outbox2[d, j] = jnp.where(j < counts[d], tile, jnp.zeros_like(tile))
            pltpu.make_async_remote_copy(
                src_ref=outbox2.at[d],
                dst_ref=inbox2.at[d],
                send_sem=send2.at[d],
                recv_sem=recv2.at[d],
                device_id={"section": section, "space": me + da * GRID_B + db},
                device_id_type=MESH,
            ).start()

        return 0

    lax.fori_loop(0, dirs, send_first, 0)
    conv_tiles(ids, w1, table1, emit_first, tiles)

    @pl.when(section == 1)
    def _():
        lax.fori_loop(0, tiles // 2, lambda i, _: (skip_copy(2 * i).wait_recv(), 0)[1], 0)
        halo_send(table3, *halo3)

    halo_receive(table2, *halo2)
    loads[2].wait()
    loads[3].wait()

    def emit_out(t, part):
        acc[t // 2] = part
        part = jnp.maximum(part, 0.0).astype(out.dtype)
        out[t] = part[:, :vox]
        out[t + 1] = part[:, vox:]

    conv_tiles(ids, w2, table2, emit_out, tiles)

    @pl.when(section == 0)
    def _():
        lax.fori_loop(0, tiles // 2, lambda i, _: (skip_copy(2 * i).wait_send(), 0)[1], 0)

    @pl.when(section == 1)
    def _():
        halo_receive(table3, *halo3)

        def emit_sum(t, part):
            part = jnp.maximum(part + acc[t // 2], 0.0).astype(out.dtype)
            out[t] = part[:, :vox]
            out[t + 1] = part[:, vox:]

        conv_tiles(ids, w3, table3, emit_sum, tiles)
        halo_sent(*halo3)

    halo_sent(*halo1)
    halo_sent(*halo2)


def local(feats, w_first, w_second, w_skip, send_tiles, send_counts, neighbours):
    ids, send_rows, counts = neighbours[0], send_tiles[0], send_counts[0]
    own = feats[0]
    tiles, channels, vox = own.shape
    dirs, cap = send_rows.shape
    table = pltpu.VMEM((tiles + dirs * cap + 1, channels, vox), own.dtype)
    weights = pltpu.VMEM(w_skip.shape, w_skip.dtype)
    box = pltpu.VMEM((dirs, cap, channels, vox), own.dtype)
    smem = pl.BlockSpec(memory_space=pltpu.SMEM)
    anywhere = pl.BlockSpec(memory_space=pltpu.HBM)
    second = pl.pallas_call(
        network,
        out_shape=jax.ShapeDtypeStruct((tiles, channels, vox), own.dtype),
        in_specs=[smem] * 3 + [anywhere] * 4,
        out_specs=pl.BlockSpec(memory_space=pltpu.VMEM),
        scratch_shapes=[table] * 3
        + [weights] * 3
        + [pltpu.VMEM((tiles // 2, channels, 2 * vox), jnp.float32)]
        + [box] * 6
        + [pltpu.SemaphoreType.DMA((4,))]
        + [pltpu.SemaphoreType.DMA((dirs,))] * 6
        + [pltpu.SemaphoreType.DMA((tiles // 2,))] * 2,
        compiler_params=pltpu.CompilerParams(
            collective_id=0, has_side_effects=True, vmem_limit_bytes=56 * 2**20
        ),
    )(ids.T, send_rows.T, counts, own, w_first[0], w_second[0], w_skip)
    return second[None]


def solution(mesh):
    placed = (
        P("section", "space", None, None),
        P("section", None, None, None),
        P("section", None, None, None),
        P(),
        P("section", "space", None),
        P("section", "space"),
        P("section", None, "space"),
    )
    return jax.shard_map(
        local,
        mesh=mesh,
        in_specs=placed,
        out_specs=P("section", "space", None, None),
        check_vma=False,
    )
```

```python
import jax
import jax.numpy as jnp
from jax import lax
from jax.experimental import pallas as pl
from jax.experimental.pallas import tpu as pltpu
from jax.sharding import PartitionSpec as P

GRID_B = 8

step_rows = (-1, -1, -1, 0, 0, 1, 1, 1)
step_cols = (-1, 0, 1, -1, 1, -1, 0, 1)


def conv_pair(ids, w, table, first, second):
    koff = w.shape[0]
    acc = None
    for i in range(0, koff, 2):
        lhs, rhs = [], []
        for k in range(i, min(i + 2, koff)):
            lhs.append(w[k])
            rhs.append(jnp.concatenate([table[ids[first, k]], table[ids[second, k]]], axis=1))
        part = jnp.dot(
            jnp.concatenate(lhs, axis=1),
            jnp.concatenate(rhs, axis=0),
            preferred_element_type=jnp.float32,
        )
        acc = part if acc is None else acc + part
    return acc


def conv_tiles(ids, w, table, emit, tiles):
    width = 8 if tiles % 8 == 0 else 2

    def body(step, _):
        firsts = [step * width + i for i in range(0, width, 2)]
        parts = [conv_pair(ids, w, table, t, t + 1) for t in firsts]
        for t, part in zip(firsts, parts):
            emit(t, part)
        return 0

    lax.fori_loop(0, tiles // width, body, 0)


MESH = pl.DeviceIdType.MESH


def network(
    ids, rows, counts, feats, w1_hbm, w2_hbm, w3_hbm, out,
    table1, table2, table3, w1, w2, w3, acc,
    outbox1, outbox2, outbox3, inbox1, inbox2, inbox3,
    local_sems, send1, recv1, send2, recv2, send3, recv3, send_skip, recv_skip,
):
    tiles, _, vox = feats.shape
    cap, dirs = rows.shape
    section = lax.axis_index("section")
    me = lax.axis_index("space")
    grid_a = lax.axis_size("space") // GRID_B
    row, col = me // GRID_B, me % GRID_B

    def inside(d, sign):
        r, c = row + sign * step_rows[d], col + sign * step_cols[d]
        return (r >= 0) & (r < grid_a) & (c >= 0) & (c < GRID_B)

    def target(d):
        return {"section": section, "space": me + step_rows[d] * GRID_B + step_cols[d]}

    sibling = {"section": 1 - section, "space": me}

    loads = [
        pltpu.make_async_copy(src, dst, local_sems.at[i])
        for i, (src, dst) in enumerate(
            [(feats, table1.at[pl.ds(0, tiles)]), (w1_hbm, w1), (w2_hbm, w2), (w3_hbm, w3)]
        )
    ]
    for load in loads:
        load.start()

    barrier = pltpu.get_barrier_semaphore()
    for d in range(dirs):

        @pl.when(inside(d, 1))
        def _():
            pl.semaphore_signal(barrier, inc=1, device_id=target(d), device_id_type=MESH)

    pl.semaphore_signal(barrier, inc=1, device_id=sibling, device_id_type=MESH)
    peers = jnp.int32(1)
    for d in range(dirs):
        peers += jnp.where(inside(d, -1), 1, 0).astype(jnp.int32)
    pl.semaphore_wait(barrier, peers)

    def halo_copy(d, outbox, inbox, send, recv):
        return pltpu.make_async_remote_copy(
            src_ref=outbox.at[d],
            dst_ref=inbox.at[d],
            send_sem=send.at[d],
            recv_sem=recv.at[d],
            device_id=target(d),
            device_id_type=MESH,
        )

    def halo_send(table, outbox, inbox, send, recv):
        for d in sorted(range(dirs), key=lambda d: step_rows[d] == 0):
            for j in range(cap):
                tile = table[rows[j, d]]
                outbox[d, j] = jnp.where(j < counts[d], tile, jnp.zeros_like(tile))

            @pl.when(inside(d, 1))
            def _():
                halo_copy(d, outbox, inbox, send, recv).start()

    def halo_receive(table, outbox, inbox, send, recv):
        for d in range(dirs):
            place = pl.ds(tiles + d * cap, cap)

            @pl.when(inside(d, -1))
            def _():
                halo_copy(d, outbox, inbox, send, recv).wait_recv()
                table[place] = inbox[d]

            @pl.when(jnp.logical_not(inside(d, -1)))
            def _():
                table[place] = jnp.zeros((cap,) + table.shape[1:], table.dtype)

        table[tiles + dirs * cap] = jnp.zeros(table.shape[1:], table.dtype)

    def halo_sent(outbox, inbox, send, recv):
        for d in range(dirs):

            @pl.when(inside(d, 1))
            def _():
                halo_copy(d, outbox, inbox, send, recv).wait_send()

    def skip_copy(t):
        return pltpu.make_async_remote_copy(
            src_ref=table2.at[pl.ds(t, 2)],
            dst_ref=table3.at[pl.ds(t, 2)],
            send_sem=send_skip.at[t // 2],
            recv_sem=recv_skip.at[t // 2],
            device_id=sibling,
            device_id_type=MESH,
        )

    halo1 = (outbox1, inbox1, send1, recv1)
    halo2 = (outbox2, inbox2, send2, recv2)
    halo3 = (outbox3, inbox3, send3, recv3)

    loads[0].wait()
    halo_send(table1, *halo1)
    halo_receive(table1, *halo1)
    loads[1].wait()

    def emit_first(t, part):
        part = jnp.maximum(part, 0.0).astype(table2.dtype)
        table2[t] = part[:, :vox]
        table2[t + 1] = part[:, vox:]

        @pl.when(section == 0)
        def _():
            skip_copy(t).start()

    def send_first(i, _):
        d = jnp.where(i < 3, i, jnp.where(i < 6, i + 2, i - 3)).astype(jnp.int32)
        step = d + jnp.where(d >= dirs // 2, 1, 0).astype(jnp.int32)
        da, db = step // 3 - 1, step % 3 - 1
        r, c = row + da, col + db

        @pl.when((r >= 0) & (r < grid_a) & (c >= 0) & (c < GRID_B))
        def _():
            part = conv_pair(ids, w1, table1, rows[0, d], rows[1, d])
            part = jnp.maximum(part, 0.0).astype(outbox2.dtype)
            for j in range(cap):
                tile = part[:, j * vox : (j + 1) * vox]
                outbox2[d, j] = jnp.where(j < counts[d], tile, jnp.zeros_like(tile))
            pltpu.make_async_remote_copy(
                src_ref=outbox2.at[d],
                dst_ref=inbox2.at[d],
                send_sem=send2.at[d],
                recv_sem=recv2.at[d],
                device_id={"section": section, "space": me + da * GRID_B + db},
                device_id_type=MESH,
            ).start()

        return 0

    lax.fori_loop(0, dirs, send_first, 0)
    conv_tiles(ids, w1, table1, emit_first, tiles)

    @pl.when(section == 1)
    def _():
        lax.fori_loop(0, tiles // 2, lambda i, _: (skip_copy(2 * i).wait_recv(), 0)[1], 0)
        halo_send(table3, *halo3)

    halo_receive(table2, *halo2)
    loads[2].wait()
    loads[3].wait()

    def emit_out(t, part):
        acc[t // 2] = part
        part = jnp.maximum(part, 0.0).astype(out.dtype)
        out[t] = part[:, :vox]
        out[t + 1] = part[:, vox:]

    conv_tiles(ids, w2, table2, emit_out, tiles)

    @pl.when(section == 0)
    def _():
        lax.fori_loop(0, tiles // 2, lambda i, _: (skip_copy(2 * i).wait_send(), 0)[1], 0)

    @pl.when(section == 1)
    def _():
        halo_receive(table3, *halo3)

        def emit_sum(t, part):
            part = jnp.maximum(part + acc[t // 2], 0.0).astype(out.dtype)
            out[t] = part[:, :vox]
            out[t + 1] = part[:, vox:]

        conv_tiles(ids, w3, table3, emit_sum, tiles)
        halo_sent(*halo3)

    halo_sent(*halo1)
    halo_sent(*halo2)


def local(feats, w_first, w_second, w_skip, send_tiles, send_counts, neighbours):
    ids, send_rows, counts = neighbours[0], send_tiles[0], send_counts[0]
    own = feats[0]
    tiles, channels, vox = own.shape
    dirs, cap = send_rows.shape
    table = pltpu.VMEM((tiles + dirs * cap + 1, channels, vox), own.dtype)
    weights = pltpu.VMEM(w_skip.shape, w_skip.dtype)
    box = pltpu.VMEM((dirs, cap, channels, vox), own.dtype)
    smem = pl.BlockSpec(memory_space=pltpu.SMEM)
    anywhere = pl.BlockSpec(memory_space=pltpu.HBM)
    second = pl.pallas_call(
        network,
        out_shape=jax.ShapeDtypeStruct((tiles, channels, vox), own.dtype),
        in_specs=[smem] * 3 + [anywhere] * 4,
        out_specs=pl.BlockSpec(memory_space=pltpu.VMEM),
        scratch_shapes=[table] * 3
        + [weights] * 3
        + [pltpu.VMEM((tiles // 2, channels, 2 * vox), jnp.float32)]
        + [box] * 6
        + [pltpu.SemaphoreType.DMA((4,))]
        + [pltpu.SemaphoreType.DMA((dirs,))] * 6
        + [pltpu.SemaphoreType.DMA((tiles // 2,))] * 2,
        compiler_params=pltpu.CompilerParams(
            collective_id=0, has_side_effects=True, vmem_limit_bytes=56 * 2**20
        ),
    )(ids.T, send_rows.T, counts, own, w_first[0], w_second[0], w_skip)
    return second[None]


def solution(mesh):
    placed = (
        P("section", "space", None, None),
        P("section", None, None, None),
        P("section", None, None, None),
        P(),
        P("section", "space", None),
        P("section", "space"),
        P("section", None, "space"),
    )
    return jax.shard_map(
        local,
        mesh=mesh,
        in_specs=placed,
        out_specs=P("section", "space", None, None),
        check_vma=False,
    )
```
